32 devices in a mesh: rows: 16 (over z, y, x), cols: 2 (over core).
Axes of the slice: x: 2, y: 2, z: 4, core: 2. Of those that a mesh axis runs over, the one named last changes fastest.
Arguments:
- matrix: float32 [4096, 4096], P('rows', 'cols'), may hold values from 0 to 250, as said below
- pivot_rows: int32 [512], replicated, may hold values from 0 to 4095, as said below
- panel_perm: int32 [512], replicated, may hold values from 0 to 511, as said below
- block_inverse: float32 [512, 512], P('rows'), may hold values from 0 to 250, as said below
Outputs:
- reduced: float32 [4096, 4096], P('rows', 'cols')
- multipliers: float32 [4096, 512], P('rows', 'cols')
- normalized: float32 [512, 4096], P('rows', 'cols')
The draws below stay inside these ranges and needn't reach their ends.
Inputs may be any that keep to these rules, and one draw needn't show every extreme that they name: `matrix`: whole numbers; the [512, 512] block of rows pivot_rows and columns panel_perm, in that order, has block_inverse as its inverse modulo 251. `pivot_rows`: 512 distinct row numbers; no more than 128 of them lie among the rows of one device along rows, and the rows of some device hold exactly 128. `panel_perm`: each number once. `block_inverse`: whole numbers.
All inputs are finite; a program needn't handle non-finite values.
Results may differ from the reference program's by a relative error of at most 0.0003.
Values may be sent and summed in bfloat16 or wider, within the bound.
A program may use at most 64 MiB of HBM per device.

```python
import jax
import jax.numpy as jnp
from jax import lax

ROWS_DEV = 256
PW = 512
NR = 4096
NC = 4096
PIVOTS_MOST = 128


def power_mod(values, exponent):
    result = jnp.ones_like(values)
    base_val = values
    while exponent > 0:
        if exponent % 2 == 1:
            result = jnp.mod(result * base_val, 251)
        base_val = jnp.mod(base_val * base_val, 251)
        exponent = exponent // 2
    return result


def unit_inverse(strict):
    identity = jnp.eye(PW, dtype=jnp.int32)
    result = jnp.mod(identity - strict, 251)
    power_now = strict
    for number in range((PW - 1).bit_length() - 1):
        power_now = jnp.mod(jnp.dot(power_now, power_now), 251)
        result = jnp.mod(jnp.dot(result, jnp.mod(identity + power_now, 251)), 251)
    return result


def panel_setup(key):
    keys = [jax.random.fold_in(key, 71 + number) for number in range(9)]
    devices_count = NR // ROWS_DEV
    slot_total = devices_count * PIVOTS_MOST
    order = jax.random.permutation(keys[0], devices_count)
    device_rank = jnp.argsort(order).astype(jnp.int32)
    flat = jnp.arange(slot_total, dtype=jnp.int32)
    slot_device = flat // PIVOTS_MOST
    slot_number = flat % PIVOTS_MOST
    rank_here = device_rank[slot_device]
    noise = jax.random.randint(keys[1], (slot_total,), 0, 64)
    score = (slot_number * (1 + rank_here % 4) * 64 + noise) * slot_total + flat
    score = jnp.where(rank_here == 0, flat - slot_total, score)
    picked = jnp.argsort(score)[:PW].astype(jnp.int32)
    picked = picked[jax.random.permutation(keys[2], PW)]
    row_orders = jax.vmap(lambda sub_key: jax.random.permutation(sub_key, ROWS_DEV))(jax.random.split(keys[3], devices_count)).astype(jnp.int32)
    pivots = picked // PIVOTS_MOST * ROWS_DEV + row_orders[picked // PIVOTS_MOST, picked % PIVOTS_MOST]
    perm = jax.random.permutation(keys[4], PW).astype(jnp.int32)
    inverses = jax.random.randint(keys[5], (PW,), 1, 251)
    diagonal = power_mod(inverses, 249)
    lower_part = jnp.tril(jax.random.randint(keys[6], (PW, PW), 0, 251), -1)
    upper_part = jnp.triu(jax.random.randint(keys[7], (PW, PW), 0, 251), 1)
    identity = jnp.eye(PW, dtype=jnp.int32)
    block = jnp.mod(jnp.dot((identity + lower_part) * diagonal[None, :], identity + upper_part), 251)
    inverse = jnp.mod(jnp.dot(unit_inverse(upper_part), jnp.mod(inverses[:, None] * unit_inverse(lower_part), 251)), 251)
    base_matrix = jax.random.randint(keys[8], (NR, NC), 0, 251)
    base_matrix = base_matrix.at[pivots[:, None], perm[None, :]].set(block)
    return (base_matrix.astype(jnp.float32), pivots, perm, inverse.astype(jnp.float32))


def draw_matrix(key, part):
    return panel_setup(key)[0]


def draw_pivot_rows(key, part):
    return panel_setup(key)[1]


def draw_panel_perm(key, part):
    return panel_setup(key)[2]


def draw_block_inverse(key, part):
    return panel_setup(key)[3]


def setup_inputs(seed: int = 0) -> dict:
    seeds = jax.random.split(jax.random.key(seed), 5)
    matrix = draw_matrix(jax.random.fold_in(seeds[4], 71), 0)
    pivot_rows = draw_pivot_rows(jax.random.fold_in(seeds[4], 71), 0)
    panel_perm = draw_panel_perm(jax.random.fold_in(seeds[4], 71), 0)
    block_inverse = draw_block_inverse(jax.random.fold_in(seeds[4], 71), 0)
    return {"matrix": matrix, "pivot_rows": pivot_rows, "panel_perm": panel_perm, "block_inverse": block_inverse}


modulus = 251.0


def mod_product(left_side, right_side):
    inner_depth = left_side.shape[1]
    stride = min(256, inner_depth)
    accumulated = jnp.zeros((left_side.shape[0], right_side.shape[1]), jnp.float32)
    for first_col in range(0, inner_depth, stride):
        partial_value = jnp.dot(left_side[:, first_col:first_col + stride], right_side[first_col:first_col + stride], preferred_element_type=jnp.float32, precision=lax.Precision.HIGHEST)
        accumulated = accumulated + jnp.mod(partial_value, modulus)
    return jnp.mod(accumulated, modulus)


def reference(matrix, pivot_rows, panel_perm, block_inverse):
    panel_cols = jnp.take(matrix[:, :PW], panel_perm, axis=0 + 1)
    multipliers = mod_product(panel_cols, block_inverse)
    pivot_slab = jnp.take(matrix, pivot_rows, axis=0)
    reduced = jnp.mod(matrix - mod_product(multipliers, pivot_slab), modulus)
    normalized = mod_product(block_inverse, pivot_slab)
    return reduced, multipliers, normalized
```

```python
import functools

import jax
import jax.numpy as jnp
from jax import lax
from jax.experimental import pallas as pl
from jax.experimental.pallas import tpu as pltpu
from jax.sharding import PartitionSpec as P

MESH = pl.DeviceIdType.MESH
MOD = 251.0
INV = 1.0 / 251.0
BLOCK = 32


def near_mod(x):
    return x - MOD * jnp.floor(x * INV)


def small_mod(x):
    return x - MOD * jnp.floor((x + 0.5) * INV)


def mod_parts(a, b):
    depth = a.shape[1]
    step = min(256, depth)
    total = None
    for k in range(0, depth, step):
        piece = near_mod(
            jnp.dot(a[:, k : k + step], b[k : k + step], preferred_element_type=jnp.float32)
        )
        total = piece if total is None else total + piece
    return total


def bit_orders(bits):
    rest = list(range(2, bits))
    return {
        "xzy": [0] + rest + [1],
        "yzx": [1] + rest + [0],
        "xyz": [0, 1] + rest,
        "yxz": [1, 0] + rest,
    }


def place_of(block, order):
    index = 0
    for b in order:
        index = index * 2 + ((block >> b) & 1)
    return index


def kernel(cfg, piv_ref, perm_ref, mat_hbm, inv_ref, red_hbm, mult_ref, norm_ref,
           mat, abuf, buf, rbuf, gbuf, lbuf, ibuf, full_inv, obuf,
           in_sem, out_sem, s_send, s_recv, g_send, g_recv, l_send, l_recv,
           i_send, i_recv, a_send, a_recv):
    R, C, bits, hbits, orders, iorders, width = (
        cfg["R"], cfg["C"], cfg["bits"], cfg["hbits"], cfg["orders"], cfg["iorders"], cfg["width"]
    )
    NB = 1 << hbits
    parts = len(orders)
    rows_here = mat.shape[0]
    pw = piv_ref.shape[1]
    r = lax.axis_index("rows")
    c = lax.axis_index("cols")
    fetch = pltpu.make_async_copy(mat_hbm, mat, in_sem)
    fetch.start()

    bit = [(r >> b) & 1 for b in range(bits)]
    partner = [r + (1 << b) * (1 - 2 * bit[b]) for b in range(bits)]

    inv_mine = inv_ref[...].astype(jnp.bfloat16)
    iw = inv_mine.shape[1] // len(iorders)
    for h, order in enumerate(iorders):
        ibuf[h, place_of(r, order)] = inv_mine[:, h * iw : (h + 1) * iw]

    barrier = pltpu.get_barrier_semaphore()
    for b in range(bits):
        pl.semaphore_signal(barrier, inc=1, device_id=(partner[b], c), device_id_type=MESH)
    for k in range(1, C):
        pl.semaphore_signal(barrier, inc=1, device_id=(r, lax.rem(c + k, C)), device_id_type=MESH)
    pl.semaphore_wait(barrier, bits + C - 1)

    def send(src, dst, ss, rs, b):
        return pltpu.make_async_remote_copy(
            src_ref=src, dst_ref=dst, send_sem=ss, recv_sem=rs,
            device_id=(partner[b], c), device_id_type=MESH,
        )

    sent = []

    def go(copy):
        copy.start()
        sent.append(copy)
        return copy

    def inv_step(h, j):
        order = iorders[h]
        b = order[bits - 1 - j]
        size = 1 << j
        base = (place_of(r, order) // size) * size
        region = ibuf.at[h, pl.ds(base, size)]
        return go(send(region, region, i_send.at[h, j], i_recv.at[h, j], b))

    iflight = [inv_step(h, 0) for h in range(len(iorders))]

    fetch.wait()

    @pl.when(c == 0)
    def _():
        abuf[...] = mat[:, :pw].astype(jnp.bfloat16)

    def panel_copy(k):
        return pltpu.make_async_remote_copy(
            src_ref=abuf, dst_ref=abuf, send_sem=a_send.at[k], recv_sem=a_recv,
            device_id=(r, k), device_id_type=MESH,
        )

    local = piv_ref[...] - r * rows_here
    pick = (
        lax.broadcasted_iota(jnp.int32, (rows_here, pw), 0) == local
    ).astype(jnp.bfloat16)
    pick = pick.T

    def lo_after(order, t):
        lo = 0
        for j in range(t):
            lo = lo + bit[order[j]] * (NB >> (j + 1))
        return lo

    roff = [0]
    for t in range(hbits):
        roff.append(roff[-1] + (NB >> (t + 1)))

    def natural(block, order):
        return place_of(block, order[:hbits])

    def slot_block(s, order):
        block = 0
        for j in range(hbits):
            block |= ((s >> (hbits - 1 - j)) & 1) << order[j]
        return block

    ranks = []
    for order in orders:
        held = sorted(range(NB), key=lambda s: slot_block(s, order))
        ranks.append(held)

    def rs_send(p, t):
        order = orders[p]
        b = order[t]
        half = NB >> (t + 1)
        away = lo_after(order, t) + (1 - bit[b]) * half
        return go(send(buf.at[p, pl.ds(away, half)], rbuf.at[p, pl.ds(roff[t], half)],
                       s_send.at[p, t], s_recv.at[p, t], b))

    flight = []
    for p in range(parts):
        chosen = jnp.dot(
            pick, mat[:, p * width : (p + 1) * width].astype(jnp.bfloat16),
            preferred_element_type=jnp.float32,
        ).astype(jnp.bfloat16)
        for i in range(NB):
            buf[p, ranks[p][i]] = chosen[i * BLOCK : (i + 1) * BLOCK]
        flight.append(rs_send(p, 0))
        if p == 1:
            for k in range(1, C):
                @pl.when(c == 0)
                def _():
                    panel_copy(k).start()

    leftover = [orders[p][hbits:] for p in range(parts)]
    for t in range(hbits):
        half = NB >> (t + 1)
        if t + 1 <= bits - 1 and t < bits - 1:
            nxt = []
            for h in range(len(iorders)):
                iflight[h].wait_recv()
                nxt.append(inv_step(h, t + 1))
            iflight = nxt
        nxt = []
        for p in range(parts):
            flight[p].wait_recv()
            keep = lo_after(orders[p], t + 1)
            value = buf[p, pl.ds(keep, half)] + rbuf[p, pl.ds(roff[t], half)]
            if t == hbits - 1:
                gbuf[p, pl.ds(keep, half)] = value
            else:
                buf[p, pl.ds(keep, half)] = value
                nxt.append(rs_send(p, t + 1))
        flight = nxt
    for j in range(hbits + 1, bits):
        nxt = []
        for h in range(len(iorders)):
            iflight[h].wait_recv()
            nxt.append(inv_step(h, j))
        iflight = nxt

    for j in range(bits - hbits):
        flight = []
        for p in range(parts):
            keep = lo_after(orders[p], hbits)
            copy = send(gbuf.at[p, keep], lbuf.at[j, p], l_send.at[p, j], l_recv.at[p, j],
                        leftover[p][j])
            copy.start()
            flight.append(copy)
        for p in range(parts):
            keep = lo_after(orders[p], hbits)
            flight[p].wait()
            gbuf[p, keep] = gbuf[p, keep] + lbuf[j, p]

    def ag_send(p, t):
        order = orders[p]
        half = NB >> (t + 1)
        region = gbuf.at[p, pl.ds(lo_after(order, t + 1), half)]
        return go(send(region, region, g_send.at[p, t], g_recv.at[p, t], order[t]))

    flight = [ag_send(p, hbits - 1) for p in range(parts)]

    for h in range(len(iorders)):
        iflight[h].wait_recv()
    irows = pw // R
    for h, order in enumerate(iorders):
        for i in range(R):
            full_inv[i * irows : (i + 1) * irows, h * iw : (h + 1) * iw] = ibuf[h, place_of(i, order)]

    @pl.when(c != 0)
    def _():
        panel_copy(0).wait_recv()

    turn = (lax.broadcasted_iota(jnp.int32, (pw, pw), 0) == perm_ref[...]).astype(jnp.bfloat16)

    for t in range(hbits - 2, -1, -1):
        nxt = []
        for p in range(parts):
            flight[p].wait_recv()
            nxt.append(ag_send(p, t))
        flight = nxt
        if t == hbits - 2:
            turned = jnp.dot(turn, full_inv[...], preferred_element_type=jnp.float32).astype(
                jnp.bfloat16
            )
            mult_ref[...] = small_mod(mod_parts(abuf[...], turned))

    outs = []
    for p in range(parts):
        flight[p].wait_recv()
        cols = slice(p * width, (p + 1) * width)
        slab = jnp.concatenate([gbuf[p, ranks[p][i]] for i in range(NB)], axis=0)
        mult = mult_ref[...].astype(jnp.bfloat16)
        obuf[p] = small_mod(mat[:, cols] - mod_parts(mult, slab))
        copy = pltpu.make_async_copy(
            obuf.at[p], red_hbm.at[:, pl.ds(p * width, width)], out_sem.at[p]
        )
        copy.start()
        outs.append(copy)
        norm_ref[:, cols] = small_mod(mod_parts(inv_mine, slab))

    for copy in outs:
        copy.wait()
    for copy in sent:
        copy.wait_send()
    for k in range(1, C):
        @pl.when(c == 0)
        def _():
            panel_copy(k).wait_send()


def body(sizes, matrix, pivot_rows, panel_perm, block_inverse):
    R, C = sizes
    rows_here, cols_here = matrix.shape
    pw = block_inverse.shape[1]
    irows = block_inverse.shape[0]
    bits = R.bit_length() - 1
    hbits = min(bits, (pw // BLOCK).bit_length() - 1)
    named = bit_orders(bits)
    names = ["xzy", "yzx", "xzy", "yzx", "xyz", "yxz", "xzy", "yzx"]
    orders = [named[n] for n in names]
    iorders = [named["xyz"], named["yxz"]]
    parts = len(orders)
    width = cols_here // parts
    NB = 1 << hbits
    left = max(1, bits - hbits)
    cfg = dict(R=R, C=C, bits=bits, hbits=hbits, orders=orders, iorders=iorders, width=width)
    dma = pltpu.SemaphoreType.DMA
    vmem = pl.BlockSpec(memory_space=pltpu.VMEM)
    hbm = pl.BlockSpec(memory_space=pl.ANY)
    bf = jnp.bfloat16
    reduced, multipliers, normalized = pl.pallas_call(
        functools.partial(kernel, cfg),
        out_shape=(
            jax.ShapeDtypeStruct((rows_here, cols_here), jnp.float32),
            jax.ShapeDtypeStruct((rows_here, pw), jnp.float32),
            jax.ShapeDtypeStruct((irows, cols_here), jnp.float32),
        ),
        in_specs=[vmem, vmem, hbm, vmem],
        out_specs=(hbm, vmem, vmem),
        scratch_shapes=[
            pltpu.VMEM((rows_here, cols_here), jnp.float32),
            pltpu.VMEM((rows_here, pw), bf),
            pltpu.VMEM((parts, NB, BLOCK, width), bf),
            pltpu.VMEM((parts, NB, BLOCK, width), bf),
            pltpu.VMEM((parts, NB, BLOCK, width), bf),
            pltpu.VMEM((left, parts, BLOCK, width), bf),
            pltpu.VMEM((len(iorders), R, irows, pw // len(iorders)), bf),
            pltpu.VMEM((pw, pw), bf),
            pltpu.VMEM((parts, rows_here, width), jnp.float32),
            dma, dma((parts,)),
            dma((parts, hbits)), dma((parts, hbits)),
            dma((parts, hbits)), dma((parts, hbits)),
            dma((parts, left)), dma((parts, left)),
            dma((len(iorders), bits)), dma((len(iorders), bits)),
            dma((C,)), dma,
        ],
        compiler_params=pltpu.CompilerParams(
            collective_id=0, has_side_effects=True, vmem_limit_bytes=48 * 1024 * 1024
        ),
    )(pivot_rows[None, :], panel_perm[None, :], matrix, block_inverse)
    share = pw // C
    mult_share = lax.dynamic_slice_in_dim(multipliers, lax.axis_index("cols") * share, share, 1)
    return reduced, mult_share, normalized


def solution(mesh):
    in_specs = (P("rows", "cols"), P(), P(), P("rows", None))
    out_specs = (P("rows", "cols"), P("rows", "cols"), P("rows", "cols"))
    sizes = (mesh.shape["rows"], mesh.shape["cols"])
    return jax.shard_map(
        functools.partial(body, sizes), mesh=mesh, in_specs=in_specs, out_specs=out_specs,
        check_vma=False,
    )
```

```python
import functools

import jax
import jax.numpy as jnp
from jax import lax
from jax.experimental import pallas as pl
from jax.experimental.pallas import tpu as pltpu
from jax.sharding import PartitionSpec as P

MESH = pl.DeviceIdType.MESH
MOD = 251.0
INV = 1.0 / 251.0
BLOCK = 32


def near_mod(x):
    return x - MOD * jnp.floor(x * INV)


def small_mod(x):
    return x - MOD * jnp.floor((x + 0.5) * INV)


def mod_parts(a, b):
    depth = a.shape[1]
    step = min(256, depth)
    total = None
    for k in range(0, depth, step):
        piece = near_mod(
            jnp.dot(a[:, k : k + step], b[k : k + step], preferred_element_type=jnp.float32)
        )
        total = piece if total is None else total + piece
    return total


def bit_orders(bits):
    rest = list(range(2, bits))
    return {
        "xyz": [0, 1] + rest,
        "yxz": [1, 0] + rest,
        "zxy": rest + [0, 1],
    }


def place_of(block, order):
    index = 0
    for b in order:
        index = index * 2 + ((block >> b) & 1)
    return index


def kernel(cfg, piv_hbm, perm_hbm, mat_hbm, inv_hbm, red_ref, mult_ref, norm_ref,
           piv_ref, perm_ref, inv_ref, mat, abuf, pack, packed, landed, buf, rbuf, gbuf, lbuf,
           ibuf, full_inv, mult_half, in_sem, s_send, s_recv, g_send, g_recv, l_send, l_recv,
           i_send, i_recv, a_send, a_recv):
    R, C, bits, hbits, orders, iorders, width, cap = (
        cfg["R"], cfg["C"], cfg["bits"], cfg["hbits"], cfg["orders"], cfg["iorders"],
        cfg["width"], cfg["cap"],
    )
    NB = 1 << hbits
    parts = len(orders)
    rows_here = mat.shape[0]
    pw = piv_ref.shape[1]
    r = lax.axis_index("rows")
    c = lax.axis_index("cols")
    fetch = [
        pltpu.make_async_copy(src, dst, in_sem.at[i])
        for i, (src, dst) in enumerate(
            [(piv_hbm, piv_ref), (inv_hbm, inv_ref), (mat_hbm, mat), (perm_hbm, perm_ref)]
        )
    ]
    for copy in fetch:
        copy.start()

    bit = [(r >> b) & 1 for b in range(bits)]
    partner = [r + (1 << b) * (1 - 2 * bit[b]) for b in range(bits)]

    barrier = pltpu.get_barrier_semaphore()
    for b in range(bits):
        pl.semaphore_signal(barrier, inc=1, device_id=(partner[b], c), device_id_type=MESH)
    for k in range(1, C):
        pl.semaphore_signal(barrier, inc=1, device_id=(r, lax.rem(c + k, C)), device_id_type=MESH)

    fetch[0].wait()
    piv = piv_ref[...]
    firsts = sorted({order[0] for order in orders})
    owners = [r] + [partner[b] for b in firsts]
    held = [(piv >= d * rows_here) & (piv < (d + 1) * rows_here) for d in owners]
    earlier = (
        lax.broadcasted_iota(jnp.int32, (pw, pw), 0) < lax.broadcasted_iota(jnp.int32, (pw, pw), 1)
    ).astype(jnp.bfloat16)
    flags = jnp.concatenate([h.astype(jnp.float32) for h in held], axis=0).astype(jnp.bfloat16)
    rank = jnp.dot(flags, earlier, preferred_element_type=jnp.float32).astype(jnp.int32)
    slot = lax.broadcasted_iota(jnp.int32, (cap, pw), 0)
    spots = [
        jnp.where((slot == rank[i : i + 1]) & held[i], 1.0, 0.0).astype(jnp.bfloat16)
        for i in range(len(owners))
    ]
    pick = jnp.where(
        lax.broadcasted_iota(jnp.int32, (rows_here, pw), 0) == piv - r * rows_here, 1.0, 0.0
    ).astype(jnp.bfloat16)
    pick_t = pick.T
    gather = jnp.dot(spots[0], pick_t, preferred_element_type=jnp.float32).astype(jnp.bfloat16)

    fetch[1].wait()
    inv_mine = inv_ref[...].astype(jnp.bfloat16)
    iw = inv_mine.shape[1] // len(iorders)
    for h, order in enumerate(iorders):
        ibuf[h, place_of(r, order)] = inv_mine[:, h * iw : (h + 1) * iw]
    fetch[2].wait()
    for p in range(parts):
        packed[p] = jnp.dot(
            gather, mat[:, p * width : (p + 1) * width].astype(jnp.bfloat16),
            preferred_element_type=jnp.float32,
        ).astype(jnp.bfloat16)

    @pl.when(c == 0)
    def _():
        abuf[...] = mat[:, :pw].astype(jnp.bfloat16)

    pl.semaphore_wait(barrier, bits + C - 1)

    def send(src, dst, ss, rs, b):
        return pltpu.make_async_remote_copy(
            src_ref=src, dst_ref=dst, send_sem=ss, recv_sem=rs,
            device_id=(partner[b], c), device_id_type=MESH,
        )

    sent = []
    flight = {}

    def go(key, copy):
        copy.start()
        sent.append(copy)
        flight[key] = copy

    def panel_copy(k):
        return pltpu.make_async_remote_copy(
            src_ref=abuf, dst_ref=abuf, send_sem=a_send.at[k], recv_sem=a_recv,
            device_id=(r, k), device_id_type=MESH,
        )

    def inv_step(h, j):
        order = iorders[h]
        if j > 0:
            flight["i", h].wait_recv()
        if j < bits:
            size = 1 << j
            base = (place_of(r, order) // size) * size
            region = ibuf.at[h, pl.ds(base, size)]
            go(("i", h), send(region, region, i_send.at[h, j], i_recv.at[h, j],
                              order[bits - 1 - j]))

    def lo_after(order, t):
        lo = 0
        for j in range(t):
            lo = lo + bit[order[j]] * (NB >> (j + 1))
        return lo

    roff = [0]
    for t in range(hbits):
        roff.append(roff[-1] + (NB >> (t + 1)))

    def slot_block(s, order):
        block = 0
        for j in range(hbits):
            block |= ((s >> (hbits - 1 - j)) & 1) << order[j]
        return block

    ranks = [sorted(range(NB), key=lambda s: slot_block(s, order)) for order in orders]

    def step(p, k):
        order = orders[p]
        cols = slice(p * width, (p + 1) * width)
        if k == 1:
            flight[p].wait_recv()
            chosen = jnp.dot(
                pick_t, mat[:, cols].astype(jnp.bfloat16), preferred_element_type=jnp.float32
            ) + jnp.dot(
                pack[firsts.index(order[0])], landed[p], preferred_element_type=jnp.float32
            )
            chosen = chosen.astype(jnp.bfloat16)
            for i in range(NB):
                buf[p, ranks[p][i]] = chosen[i * BLOCK : (i + 1) * BLOCK]
        elif 1 < k <= hbits:
            flight[p].wait_recv()
            t = k - 1
            half = NB >> k
            keep = lo_after(order, k)
            value = buf[p, pl.ds(keep, half)] + rbuf[p, pl.ds(roff[t], half)]
            if k == hbits:
                gbuf[p, pl.ds(keep, half)] = value
            else:
                buf[p, pl.ds(keep, half)] = value
        elif k > hbits:
            flight[p].wait_recv()
        if k == 0:
            go(p, send(packed.at[p], landed.at[p], s_send.at[p, 0], s_recv.at[p, 0], order[0]))
        elif k < hbits:
            half = NB >> (k + 1)
            away = lo_after(order, k) + (1 - bit[order[k]]) * half
            go(p, send(buf.at[p, pl.ds(away, half)], rbuf.at[p, pl.ds(roff[k], half)],
                       s_send.at[p, k], s_recv.at[p, k], order[k]))
        elif k < 2 * hbits:
            if k == hbits:
                keep = lo_after(order, hbits)
                for j, b in enumerate(order[hbits:]):
                    copy = send(gbuf.at[p, keep], lbuf.at[j, p], l_send.at[p, j],
                                l_recv.at[p, j], b)
                    copy.start()
                    copy.wait()
                    gbuf[p, keep] = gbuf[p, keep] + lbuf[j, p]
            t = 2 * hbits - 1 - k
            region = gbuf.at[p, pl.ds(lo_after(order, t + 1), NB >> (t + 1))]
            go(p, send(region, region, g_send.at[p, t], g_recv.at[p, t], order[t]))
        else:
            slab = jnp.concatenate([gbuf[p, ranks[p][i]] for i in range(NB)], axis=0)
            red_ref[:, cols] = small_mod(mat[:, cols] - mod_parts(mult_half[...], slab))
            norm_ref[:, cols] = small_mod(mod_parts(inv_mine, slab))

    def multipliers():
        irows = pw // R
        for h, order in enumerate(iorders):
            for i in range(R):
                full_inv[i * irows : (i + 1) * irows, h * iw : (h + 1) * iw] = ibuf[
                    h, place_of(i, order)
                ]

        @pl.when(c != 0)
        def _():
            panel_copy(0).wait_recv()

        fetch[3].wait()
        turn = jnp.where(
            lax.broadcasted_iota(jnp.int32, (pw, pw), 0) == perm_ref[...], 1.0, 0.0
        ).astype(jnp.bfloat16)
        turned = jnp.dot(turn, full_inv[...], preferred_element_type=jnp.float32)
        mult = small_mod(mod_parts(abuf[...], turned.astype(jnp.bfloat16)))
        mult_ref[...] = mult
        mult_half[...] = mult.astype(jnp.bfloat16)

    for event in cfg["events"]:
        if event[0] == "i":
            inv_step(event[1], event[2])
        elif event[0] == "a":
            for k in range(1, C):
                @pl.when(c == 0)
                def _():
                    panel_copy(k).start()
        elif event[0] == "u":
            for i in range(len(firsts)):
                pack[i] = spots[i + 1].T
        elif event[0] == "m":
            multipliers()
        else:
            step(event[1], event[2])

    for copy in sent:
        copy.wait_send()
    for k in range(1, C):
        @pl.when(c == 0)
        def _():
            panel_copy(k).wait_send()


def schedule(parts, halves, bits, hbits):
    events = [("i", h, 0) for h in range(halves)]
    events += [("s", p, 0) for p in range(parts)] + [("a",), ("u",)]
    for k in range(1, 2 * hbits + 1):
        if k <= bits:
            events += [("i", h, k) for h in range(halves)]
        if k == 2 * hbits:
            events += [("i", h, j) for j in range(k + 1, bits + 1) for h in range(halves)]
            events.append(("m",))
        events += [("s", p, k) for p in range(parts)]
        if k == bits + 1 and k < 2 * hbits:
            events.append(("m",))
    seen = False
    out = []
    for event in events:
        if event[0] == "m":
            if seen:
                continue
            seen = True
        out.append(event)
    return out


def body(sizes, matrix, pivot_rows, panel_perm, block_inverse):
    R, C = sizes
    rows_here, cols_here = matrix.shape
    pw = block_inverse.shape[1]
    irows = block_inverse.shape[0]
    bits = R.bit_length() - 1
    hbits = min(bits, (pw // BLOCK).bit_length() - 1)
    named = bit_orders(bits)
    names = ["xyz", "yxz", "zxy", "xyz", "yxz", "zxy", "xyz", "yxz"]
    orders = [named[n] for n in names]
    iorders = [named["xyz"], named["yxz"]]
    parts = len(orders)
    width = cols_here // parts
    NB = 1 << hbits
    left = max(1, bits - hbits)
    cap = min(rows_here, 4 * pw // R)
    firsts = len({order[0] for order in orders})
    cfg = dict(R=R, C=C, bits=bits, hbits=hbits, orders=orders, iorders=iorders, width=width,
               cap=cap, events=schedule(parts, len(iorders), bits, hbits))
    dma = pltpu.SemaphoreType.DMA
    vmem = pl.BlockSpec(memory_space=pltpu.VMEM)
    hbm = pl.BlockSpec(memory_space=pltpu.HBM)
    bf = jnp.bfloat16
    reduced, multipliers, normalized = pl.pallas_call(
        functools.partial(kernel, cfg),
        out_shape=(
            jax.ShapeDtypeStruct((rows_here, cols_here), jnp.float32),
            jax.ShapeDtypeStruct((rows_here, pw), jnp.float32),
            jax.ShapeDtypeStruct((irows, cols_here), jnp.float32),
        ),
        in_specs=[hbm, hbm, hbm, hbm],
        out_specs=(vmem, vmem, vmem),
        scratch_shapes=[
            pltpu.VMEM((1, pw), jnp.int32),
            pltpu.VMEM((1, pw), jnp.int32),
            pltpu.VMEM((irows, pw), jnp.float32),
            pltpu.VMEM((rows_here, cols_here), jnp.float32),
            pltpu.VMEM((rows_here, pw), bf),
            pltpu.VMEM((firsts, pw, cap), bf),
            pltpu.VMEM((parts, cap, width), bf),
            pltpu.VMEM((parts, cap, width), bf),
            pltpu.VMEM((parts, NB, BLOCK, width), bf),
            pltpu.VMEM((parts, NB, BLOCK, width), bf),
            pltpu.VMEM((parts, NB, BLOCK, width), bf),
            pltpu.VMEM((left, parts, BLOCK, width), bf),
            pltpu.VMEM((len(iorders), R, irows, pw // len(iorders)), bf),
            pltpu.VMEM((pw, pw), bf),
            pltpu.VMEM((rows_here, pw), bf),
            dma((4,)),
            dma((parts, hbits)), dma((parts, hbits)),
            dma((parts, hbits)), dma((parts, hbits)),
            dma((parts, left)), dma((parts, left)),
            dma((len(iorders), bits)), dma((len(iorders), bits)),
            dma((C,)), dma,
        ],
        compiler_params=pltpu.CompilerParams(
            collective_id=0, has_side_effects=True, vmem_limit_bytes=48 * 1024 * 1024
        ),
    )(pivot_rows[None, :], panel_perm[None, :], matrix, block_inverse)
    share = pw // C
    mult_share = lax.dynamic_slice_in_dim(multipliers, lax.axis_index("cols") * share, share, 1)
    return reduced, mult_share, normalized


def solution(mesh):
    in_specs = (P("rows", "cols"), P(), P(), P("rows", None))
    out_specs = (P("rows", "cols"), P("rows", "cols"), P("rows", "cols"))
    sizes = (mesh.shape["rows"], mesh.shape["cols"])
    return jax.shard_map(
        functools.partial(body, sizes), mesh=mesh, in_specs=in_specs, out_specs=out_specs,
        check_vma=False,
    )
```

```python
import functools

import jax
import jax.numpy as jnp
from jax import lax
from jax.experimental import pallas as pl
from jax.experimental.pallas import tpu as pltpu
from jax.sharding import PartitionSpec as P

MESH = pl.DeviceIdType.MESH
MOD = 251.0
INV = 1.0 / 251.0
BLOCK = 32


def near_mod(x):
    return x - MOD * jnp.floor(x * INV)


def small_mod(x):
    return x - MOD * jnp.floor((x + 0.5) * INV)


def mod_parts(a, b):
    depth = a.shape[1]
    step = min(256, depth)
    total = None
    for k in range(0, depth, step):
        piece = near_mod(
            jnp.dot(a[:, k : k + step], b[k : k + step], preferred_element_type=jnp.float32)
        )
        total = piece if total is None else total + piece
    return total


def bit_orders(bits):
    rest = list(range(2, bits))
    return {
        "xyz": [0, 1] + rest,
        "yxz": [1, 0] + rest,
        "zxy": rest + [0, 1],
    }


def place_of(block, order):
    index = 0
    for b in order:
        index = index * 2 + ((block >> b) & 1)
    return index


def kernel(cfg, piv_hbm, perm_hbm, mat_hbm, inv_hbm, red_ref, mult_ref, norm_ref,
           piv_ref, perm_ref, inv_ref, mat, abuf, pack, packed, landed, buf, rbuf, gbuf, lbuf,
           ibuf, full_inv, mult_all, mult_half, in_sem, s_send, s_recv, g_send, g_recv, l_send, l_recv,
           i_send, i_recv, a_send, a_recv, m_send, m_recv):
    R, C, bits, hbits, orders, iorders, width, cap = (
        cfg["R"], cfg["C"], cfg["bits"], cfg["hbits"], cfg["orders"], cfg["iorders"],
        cfg["width"], cfg["cap"],
    )
    NB = 1 << hbits
    parts = len(orders)
    rows_here = mat.shape[0]
    pw = piv_ref.shape[1]
    r = lax.axis_index("rows")
    c = lax.axis_index("cols")
    fetch = [
        pltpu.make_async_copy(src, dst, in_sem.at[i])
        for i, (src, dst) in enumerate(
            [(piv_hbm, piv_ref), (inv_hbm, inv_ref), (mat_hbm, mat), (perm_hbm, perm_ref)]
        )
    ]
    for copy in fetch:
        copy.start()

    bit = [(r >> b) & 1 for b in range(bits)]
    partner = [r + (1 << b) * (1 - 2 * bit[b]) for b in range(bits)]

    barrier = pltpu.get_barrier_semaphore()
    for b in range(bits):
        pl.semaphore_signal(barrier, inc=1, device_id=(partner[b], c), device_id_type=MESH)
    for k in range(1, C):
        pl.semaphore_signal(barrier, inc=1, device_id=(r, lax.rem(c + k, C)), device_id_type=MESH)

    fetch[0].wait()
    piv = piv_ref[...]
    firsts = sorted({order[0] for order in orders})
    owners = [r] + [partner[b] for b in firsts]
    held = [(piv >= d * rows_here) & (piv < (d + 1) * rows_here) for d in owners]
    earlier = (
        lax.broadcasted_iota(jnp.int32, (pw, pw), 0) < lax.broadcasted_iota(jnp.int32, (pw, pw), 1)
    ).astype(jnp.bfloat16)
    flags = jnp.concatenate([h.astype(jnp.float32) for h in held], axis=0).astype(jnp.bfloat16)
    rank = jnp.dot(flags, earlier, preferred_element_type=jnp.float32).astype(jnp.int32)
    slot = lax.broadcasted_iota(jnp.int32, (cap, pw), 0)
    spots = [
        jnp.where((slot == rank[i : i + 1]) & held[i], 1.0, 0.0).astype(jnp.bfloat16)
        for i in range(len(owners))
    ]
    pick = jnp.where(
        lax.broadcasted_iota(jnp.int32, (rows_here, pw), 0) == piv - r * rows_here, 1.0, 0.0
    ).astype(jnp.bfloat16)
    pick_t = pick.T
    gather = jnp.dot(spots[0], pick_t, preferred_element_type=jnp.float32).astype(jnp.bfloat16)

    fetch[1].wait()
    inv_mine = inv_ref[...].astype(jnp.bfloat16)
    share = pw // C
    own = inv_mine[:, :share]
    for k in range(1, C):
        own = jnp.where(c == k, inv_mine[:, k * share : (k + 1) * share], own)
    iw = share // len(iorders)
    for h, order in enumerate(iorders):
        ibuf[h, place_of(r, order)] = own[:, h * iw : (h + 1) * iw]
    fetch[2].wait()
    for p in range(parts):
        packed[p] = jnp.dot(
            gather, mat[:, p * width : (p + 1) * width].astype(jnp.bfloat16),
            preferred_element_type=jnp.float32,
        ).astype(jnp.bfloat16)

    @pl.when(c == 0)
    def _():
        abuf[...] = mat[:, :pw].astype(jnp.bfloat16)

    pl.semaphore_wait(barrier, bits + C - 1)

    def send(src, dst, ss, rs, b):
        return pltpu.make_async_remote_copy(
            src_ref=src, dst_ref=dst, send_sem=ss, recv_sem=rs,
            device_id=(partner[b], c), device_id_type=MESH,
        )

    sent = []
    flight = {}

    def go(key, copy):
        copy.start()
        sent.append(copy)
        flight[key] = copy

    def panel_copy(k):
        return pltpu.make_async_remote_copy(
            src_ref=abuf, dst_ref=abuf, send_sem=a_send.at[k], recv_sem=a_recv,
            device_id=(r, k), device_id_type=MESH,
        )

    def inv_step(h, j):
        order = iorders[h]
        if j > 0:
            flight["i", h].wait_recv()
        if j < bits:
            size = 1 << j
            base = (place_of(r, order) // size) * size
            region = ibuf.at[h, pl.ds(base, size)]
            go(("i", h), send(region, region, i_send.at[h, j], i_recv.at[h, j],
                              order[bits - 1 - j]))

    def lo_after(order, t):
        lo = 0
        for j in range(t):
            lo = lo + bit[order[j]] * (NB >> (j + 1))
        return lo

    roff = [0]
    for t in range(hbits):
        roff.append(roff[-1] + (NB >> (t + 1)))

    def slot_block(s, order):
        block = 0
        for j in range(hbits):
            block |= ((s >> (hbits - 1 - j)) & 1) << order[j]
        return block

    ranks = [sorted(range(NB), key=lambda s: slot_block(s, order)) for order in orders]

    def step(p, k):
        order = orders[p]
        cols = slice(p * width, (p + 1) * width)
        if k == 1:
            flight[p].wait_recv()
            chosen = jnp.dot(
                pick_t, mat[:, cols].astype(jnp.bfloat16), preferred_element_type=jnp.float32
            ) + jnp.dot(
                pack[firsts.index(order[0])], landed[p], preferred_element_type=jnp.float32
            )
            chosen = chosen.astype(jnp.bfloat16)
            for i in range(NB):
                buf[p, ranks[p][i]] = chosen[i * BLOCK : (i + 1) * BLOCK]
        elif 1 < k <= hbits:
            flight[p].wait_recv()
            t = k - 1
            half = NB >> k
            keep = lo_after(order, k)
            value = buf[p, pl.ds(keep, half)] + rbuf[p, pl.ds(roff[t], half)]
            if k == hbits:
                gbuf[p, pl.ds(keep, half)] = value
            else:
                buf[p, pl.ds(keep, half)] = value
        elif k > hbits:
            flight[p].wait_recv()
        if k == 0:
            go(p, send(packed.at[p], landed.at[p], s_send.at[p, 0], s_recv.at[p, 0], order[0]))
        elif k < hbits:
            half = NB >> (k + 1)
            away = lo_after(order, k) + (1 - bit[order[k]]) * half
            go(p, send(buf.at[p, pl.ds(away, half)], rbuf.at[p, pl.ds(roff[k], half)],
                       s_send.at[p, k], s_recv.at[p, k], order[k]))
        elif k < 2 * hbits:
            if k == hbits:
                keep = lo_after(order, hbits)
                for j, b in enumerate(order[hbits:]):
                    copy = send(gbuf.at[p, keep], lbuf.at[j, p], l_send.at[p, j],
                                l_recv.at[p, j], b)
                    copy.start()
                    copy.wait()
                    gbuf[p, keep] = gbuf[p, keep] + lbuf[j, p]
            t = 2 * hbits - 1 - k
            region = gbuf.at[p, pl.ds(lo_after(order, t + 1), NB >> (t + 1))]
            go(p, send(region, region, g_send.at[p, t], g_recv.at[p, t], order[t]))
        else:
            slab = jnp.concatenate([gbuf[p, ranks[p][i]] for i in range(NB)], axis=0)
            red_ref[:, cols] = small_mod(mat[:, cols] - mod_parts(mult_half[...], slab))
            norm_ref[:, cols] = small_mod(mod_parts(inv_mine, slab))

    def multipliers():
        irows = pw // R
        for h, order in enumerate(iorders):
            for i in range(R):
                full_inv[i * irows : (i + 1) * irows, h * iw : (h + 1) * iw] = ibuf[
                    h, place_of(i, order)
                ]

        @pl.when(c != 0)
        def _():
            panel_copy(0).wait_recv()

        fetch[3].wait()
        turn = jnp.where(
            lax.broadcasted_iota(jnp.int32, (pw, pw), 0) == perm_ref[...], 1.0, 0.0
        ).astype(jnp.bfloat16)
        turned = jnp.dot(turn, full_inv[...], preferred_element_type=jnp.float32)
        mult = small_mod(mod_parts(abuf[...], turned.astype(jnp.bfloat16)))
        mult_ref[...] = mult
        mult_all[c] = mult.astype(jnp.bfloat16)
        for k in range(1, C):
            swap(k).start()

    def swap(k):
        return pltpu.make_async_remote_copy(
            src_ref=mult_all.at[c], dst_ref=mult_all.at[c], send_sem=m_send.at[k],
            recv_sem=m_recv.at[k], device_id=(r, lax.rem(c + k, C)), device_id_type=MESH,
        )

    def join():
        for k in range(1, C):
            swap(k).wait()
        for k in range(C):
            mult_half[:, k * share : (k + 1) * share] = mult_all[k]

    for event in cfg["events"]:
        if event[0] == "i":
            inv_step(event[1], event[2])
        elif event[0] == "a":
            for k in range(1, C):
                @pl.when(c == 0)
                def _():
                    panel_copy(k).start()
        elif event[0] == "u":
            for i in range(len(firsts)):
                pack[i] = spots[i + 1].T
        elif event[0] == "m":
            multipliers()
        elif event[0] == "j":
            join()
        else:
            step(event[1], event[2])

    for copy in sent:
        copy.wait_send()
    for k in range(1, C):
        @pl.when(c == 0)
        def _():
            panel_copy(k).wait_send()


def schedule(parts, halves, bits, hbits):
    events = [("i", h, 0) for h in range(halves)]
    events += [("s", p, 0) for p in range(parts)] + [("a",), ("u",)]
    for k in range(1, 2 * hbits + 1):
        if k <= bits:
            events += [("i", h, k) for h in range(halves)]
        if k == 2 * hbits:
            events += [("i", h, j) for j in range(k + 1, bits + 1) for h in range(halves)]
            events += [("m",), ("j",)]
        events += [("s", p, k) for p in range(parts)]
        if k == bits + 1 and k < 2 * hbits:
            events.append(("m",))
    seen = False
    out = []
    for event in events:
        if event[0] == "m":
            if seen:
                continue
            seen = True
        out.append(event)
    return out


def put_out(*refs):
    sems = refs[6]
    copies = [pltpu.make_async_copy(refs[i], refs[3 + i], sems.at[i]) for i in range(3)]
    for copy in copies:
        copy.start()
    for copy in copies:
        copy.wait()


def body(sizes, matrix, pivot_rows, panel_perm, block_inverse):
    R, C = sizes
    rows_here, cols_here = matrix.shape
    pw = block_inverse.shape[1]
    irows = block_inverse.shape[0]
    bits = R.bit_length() - 1
    hbits = min(bits, (pw // BLOCK).bit_length() - 1)
    named = bit_orders(bits)
    names = ["xyz", "yxz", "zxy", "xyz", "yxz", "zxy", "xyz", "yxz"]
    orders = [named[n] for n in names]
    iorders = [named["xyz"], named["yxz"]]
    parts = len(orders)
    width = cols_here // parts
    NB = 1 << hbits
    share = pw // C
    left = max(1, bits - hbits)
    cap = min(rows_here, 4 * pw // R)
    firsts = len({order[0] for order in orders})
    cfg = dict(R=R, C=C, bits=bits, hbits=hbits, orders=orders, iorders=iorders, width=width,
               cap=cap, events=schedule(parts, len(iorders), bits, hbits))
    dma = pltpu.SemaphoreType.DMA
    vmem = pl.BlockSpec(memory_space=pltpu.VMEM)
    hbm = pl.BlockSpec(memory_space=pltpu.HBM)
    bf = jnp.bfloat16
    reduced, multipliers, normalized = pl.pallas_call(
        functools.partial(kernel, cfg),
        out_shape=(
            jax.ShapeDtypeStruct((rows_here, cols_here), jnp.float32),
            jax.ShapeDtypeStruct((rows_here, share), jnp.float32),
            jax.ShapeDtypeStruct((irows, cols_here), jnp.float32),
        ),
        in_specs=[hbm, hbm, hbm, hbm],
        out_specs=(vmem, vmem, vmem),
        scratch_shapes=[
            pltpu.VMEM((1, pw), jnp.int32),
            pltpu.VMEM((1, pw), jnp.int32),
            pltpu.VMEM((irows, pw), jnp.float32),
            pltpu.VMEM((rows_here, cols_here), jnp.float32),
            pltpu.VMEM((rows_here, pw), bf),
            pltpu.VMEM((firsts, pw, cap), bf),
            pltpu.VMEM((parts, cap, width), bf),
            pltpu.VMEM((parts, cap, width), bf),
            pltpu.VMEM((parts, NB, BLOCK, width), bf),
            pltpu.VMEM((parts, NB, BLOCK, width), bf),
            pltpu.VMEM((parts, NB, BLOCK, width), bf),
            pltpu.VMEM((left, parts, BLOCK, width), bf),
            pltpu.VMEM((len(iorders), R, irows, share // len(iorders)), bf),
            pltpu.VMEM((pw, share), bf),
            pltpu.VMEM((C, rows_here, share), bf),
            pltpu.VMEM((rows_here, pw), bf),
            dma((4,)),
            dma((parts, hbits)), dma((parts, hbits)),
            dma((parts, hbits)), dma((parts, hbits)),
            dma((parts, left)), dma((parts, left)),
            dma((len(iorders), bits)), dma((len(iorders), bits)),
            dma((C,)), dma, dma((C,)), dma((C,)),
        ],
        compiler_params=pltpu.CompilerParams(
            collective_id=0, has_side_effects=True, vmem_limit_bytes=48 * 1024 * 1024
        ),
    )(*[
        pltpu.with_memory_space_constraint(x, pltpu.HBM)
        for x in (pivot_rows[None, :], panel_perm[None, :], matrix, block_inverse)
    ])
    results = (reduced, multipliers, normalized)
    return pl.pallas_call(
        put_out,
        out_shape=tuple(pltpu.HBM(x.shape, x.dtype) for x in results),
        in_specs=[vmem] * 3,
        out_specs=(hbm,) * 3,
        scratch_shapes=[dma((3,))],
    )(*results)


def solution(mesh):
    in_specs = (P("rows", "cols"), P(), P(), P("rows", None))
    out_specs = (P("rows", "cols"), P("rows", "cols"), P("rows", "cols"))
    sizes = (mesh.shape["rows"], mesh.shape["cols"])
    return jax.shard_map(
        functools.partial(body, sizes), mesh=mesh, in_specs=in_specs, out_specs=out_specs,
        check_vma=False,
    )
```

```python
import functools

import jax
import jax.numpy as jnp
from jax import lax
from jax.experimental import pallas as pl
from jax.experimental.pallas import tpu as pltpu
from jax.sharding import PartitionSpec as P

MESH = pl.DeviceIdType.MESH
MOD = 251.0
INV = 1.0 / 251.0
BLOCK = 32


def near_mod(x):
    return x - MOD * jnp.floor(x * INV)


def small_mod(x):
    return x - MOD * jnp.floor((x + 0.5) * INV)


def mod_parts(a, b):
    depth = a.shape[1]
    step = min(256, depth)
    total = None
    for k in range(0, depth, step):
        piece = near_mod(
            jnp.dot(a[:, k : k + step], b[k : k + step], preferred_element_type=jnp.float32)
        )
        total = piece if total is None else total + piece
    return total


def bit_orders(bits):
    rest = list(range(2, bits))
    return {
        "xyz": [0, 1] + rest,
        "yxz": [1, 0] + rest,
        "zxy": rest + [0, 1],
    }


def place_of(block, order):
    index = 0
    for b in order:
        index = index * 2 + ((block >> b) & 1)
    return index


def kernel(cfg, piv_hbm, perm_hbm, mat_hbm, inv_hbm, red_ref, mult_ref, norm_ref,
           piv_ref, perm_ref, inv_ref, mat, abuf, pack, packed, landed, buf, rbuf, gbuf, lbuf,
           ibuf, full_inv, mult_all, mult_half, in_sem, s_send, s_recv, g_send, g_recv, l_send, l_recv,
           i_send, i_recv, a_send, a_recv, m_send, m_recv):
    R, C, bits, hbits, orders, iorders, width, cap = (
        cfg["R"], cfg["C"], cfg["bits"], cfg["hbits"], cfg["orders"], cfg["iorders"],
        cfg["width"], cfg["cap"],
    )
    NB = 1 << hbits
    parts = len(orders)
    rows_here = mat.shape[0]
    pw = piv_ref.shape[1]
    r = lax.axis_index("rows")
    c = lax.axis_index("cols")
    fetch = [
        pltpu.make_async_copy(src, dst, in_sem.at[i])
        for i, (src, dst) in enumerate(
            [(piv_hbm, piv_ref), (inv_hbm, inv_ref), (perm_hbm, perm_ref)]
            + [
                (mat_hbm.at[:, pl.ds(p * width, width)], mat.at[:, pl.ds(p * width, width)])
                for p in range(parts)
            ]
        )
    ]
    for copy in fetch:
        copy.start()

    bit = [(r >> b) & 1 for b in range(bits)]
    partner = [r + (1 << b) * (1 - 2 * bit[b]) for b in range(bits)]

    barrier = pltpu.get_barrier_semaphore()
    for b in range(bits):
        pl.semaphore_signal(barrier, inc=1, device_id=(partner[b], c), device_id_type=MESH)
    for k in range(1, C):
        pl.semaphore_signal(barrier, inc=1, device_id=(r, lax.rem(c + k, C)), device_id_type=MESH)

    fetch[0].wait()
    piv = piv_ref[...]
    firsts = sorted({order[0] for order in orders})
    owners = [r] + [partner[b] for b in firsts]
    held = [(piv >= d * rows_here) & (piv < (d + 1) * rows_here) for d in owners]
    earlier = (
        lax.broadcasted_iota(jnp.int32, (pw, pw), 0) < lax.broadcasted_iota(jnp.int32, (pw, pw), 1)
    ).astype(jnp.bfloat16)
    flags = jnp.concatenate([h.astype(jnp.float32) for h in held], axis=0).astype(jnp.bfloat16)
    rank = jnp.dot(flags, earlier, preferred_element_type=jnp.float32).astype(jnp.int32)
    slot = lax.broadcasted_iota(jnp.int32, (cap, pw), 0)
    spots = [
        jnp.where((slot == rank[i : i + 1]) & held[i], 1.0, 0.0).astype(jnp.bfloat16)
        for i in range(len(owners))
    ]
    pick = jnp.where(
        lax.broadcasted_iota(jnp.int32, (rows_here, pw), 0) == piv - r * rows_here, 1.0, 0.0
    ).astype(jnp.bfloat16)
    pick_t = pick.T
    gather = jnp.dot(spots[0], pick_t, preferred_element_type=jnp.float32).astype(jnp.bfloat16)

    fetch[1].wait()
    inv_mine = inv_ref[...].astype(jnp.bfloat16)
    share = pw // C
    own = inv_mine[:, :share]
    for k in range(1, C):
        own = jnp.where(c == k, inv_mine[:, k * share : (k + 1) * share], own)
    iw = share // len(iorders)
    for h, order in enumerate(iorders):
        ibuf[h, place_of(r, order)] = own[:, h * iw : (h + 1) * iw]
    pl.semaphore_wait(barrier, bits + C - 1)

    def send(src, dst, ss, rs, b):
        return pltpu.make_async_remote_copy(
            src_ref=src, dst_ref=dst, send_sem=ss, recv_sem=rs,
            device_id=(partner[b], c), device_id_type=MESH,
        )

    sent = []
    flight = {}

    def go(key, copy):
        copy.start()
        sent.append(copy)
        flight[key] = copy

    def panel_copy(k):
        return pltpu.make_async_remote_copy(
            src_ref=abuf, dst_ref=abuf, send_sem=a_send.at[k], recv_sem=a_recv,
            device_id=(r, k), device_id_type=MESH,
        )

    def inv_step(h, j):
        order = iorders[h]
        if j > 0:
            flight["i", h].wait_recv()
        if j < bits:
            size = 1 << j
            base = (place_of(r, order) // size) * size
            region = ibuf.at[h, pl.ds(base, size)]
            go(("i", h), send(region, region, i_send.at[h, j], i_recv.at[h, j],
                              order[bits - 1 - j]))

    def lo_after(order, t):
        lo = 0
        for j in range(t):
            lo = lo + bit[order[j]] * (NB >> (j + 1))
        return lo

    roff = [0]
    for t in range(hbits):
        roff.append(roff[-1] + (NB >> (t + 1)))

    def slot_block(s, order):
        block = 0
        for j in range(hbits):
            block |= ((s >> (hbits - 1 - j)) & 1) << order[j]
        return block

    ranks = [sorted(range(NB), key=lambda s: slot_block(s, order)) for order in orders]

    def step(p, k):
        order = orders[p]
        cols = slice(p * width, (p + 1) * width)
        if k == 1:
            flight[p].wait_recv()
            chosen = jnp.dot(
                pick_t, mat[:, cols].astype(jnp.bfloat16), preferred_element_type=jnp.float32
            ) + jnp.dot(
                pack[firsts.index(order[0])], landed[p], preferred_element_type=jnp.float32
            )
            chosen = chosen.astype(jnp.bfloat16)
            for i in range(NB):
                buf[p, ranks[p][i]] = chosen[i * BLOCK : (i + 1) * BLOCK]
        elif 1 < k <= hbits:
            flight[p].wait_recv()
            t = k - 1
            half = NB >> k
            keep = lo_after(order, k)
            value = buf[p, pl.ds(keep, half)] + rbuf[p, pl.ds(roff[t], half)]
            if k == hbits:
                gbuf[p, pl.ds(keep, half)] = value
            else:
                buf[p, pl.ds(keep, half)] = value
        elif k > hbits:
            flight[p].wait_recv()
        if k == 0:
            fetch[3 + p].wait()
            packed[p] = jnp.dot(
                gather, mat[:, cols].astype(jnp.bfloat16), preferred_element_type=jnp.float32
            ).astype(jnp.bfloat16)
            go(p, send(packed.at[p], landed.at[p], s_send.at[p, 0], s_recv.at[p, 0], order[0]))
        elif k < hbits:
            half = NB >> (k + 1)
            away = lo_after(order, k) + (1 - bit[order[k]]) * half
            go(p, send(buf.at[p, pl.ds(away, half)], rbuf.at[p, pl.ds(roff[k], half)],
                       s_send.at[p, k], s_recv.at[p, k], order[k]))
        elif k < 2 * hbits:
            if k == hbits:
                keep = lo_after(order, hbits)
                for j, b in enumerate(order[hbits:]):
                    copy = send(gbuf.at[p, keep], lbuf.at[j, p], l_send.at[p, j],
                                l_recv.at[p, j], b)
                    copy.start()
                    copy.wait()
                    gbuf[p, keep] = gbuf[p, keep] + lbuf[j, p]
            t = 2 * hbits - 1 - k
            region = gbuf.at[p, pl.ds(lo_after(order, t + 1), NB >> (t + 1))]
            go(p, send(region, region, g_send.at[p, t], g_recv.at[p, t], order[t]))
        else:
            slab = jnp.concatenate([gbuf[p, ranks[p][i]] for i in range(NB)], axis=0)
            red_ref[:, cols] = small_mod(mat[:, cols] - mod_parts(mult_half[...], slab))
            norm_ref[:, cols] = small_mod(mod_parts(inv_mine, slab))

    def multipliers():
        irows = pw // R
        for h, order in enumerate(iorders):
            for i in range(R):
                full_inv[i * irows : (i + 1) * irows, h * iw : (h + 1) * iw] = ibuf[
                    h, place_of(i, order)
                ]

        @pl.when(c != 0)
        def _():
            panel_copy(0).wait_recv()

        fetch[2].wait()
        turn = jnp.where(
            lax.broadcasted_iota(jnp.int32, (pw, pw), 0) == perm_ref[...], 1.0, 0.0
        ).astype(jnp.bfloat16)
        turned = jnp.dot(turn, full_inv[...], preferred_element_type=jnp.float32)
        mult = small_mod(mod_parts(abuf[...], turned.astype(jnp.bfloat16)))
        mult_ref[...] = mult
        mult_all[c] = mult.astype(jnp.bfloat16)
        for k in range(1, C):
            swap(k).start()

    def swap(k):
        return pltpu.make_async_remote_copy(
            src_ref=mult_all.at[c], dst_ref=mult_all.at[c], send_sem=m_send.at[k],
            recv_sem=m_recv.at[k], device_id=(r, lax.rem(c + k, C)), device_id_type=MESH,
        )

    def join():
        for k in range(1, C):
            swap(k).wait()
        for k in range(C):
            mult_half[:, k * share : (k + 1) * share] = mult_all[k]

    for event in cfg["events"]:
        if event[0] == "i":
            inv_step(event[1], event[2])
        elif event[0] == "a":
            @pl.when(c == 0)
            def _():
                abuf[...] = mat[:, :pw].astype(jnp.bfloat16)

            for k in range(1, C):
                @pl.when(c == 0)
                def _():
                    panel_copy(k).start()
        elif event[0] == "u":
            for i in range(len(firsts)):
                pack[i] = spots[i + 1].T
        elif event[0] == "m":
            multipliers()
        elif event[0] == "j":
            join()
        else:
            step(event[1], event[2])

    for copy in sent:
        copy.wait_send()
    for k in range(1, C):
        @pl.when(c == 0)
        def _():
            panel_copy(k).wait_send()


def schedule(parts, halves, bits, hbits):
    events = [("i", h, 0) for h in range(halves)]
    events += [("s", p, 0) for p in range(parts)] + [("a",), ("u",)]
    for k in range(1, 2 * hbits + 1):
        if k <= bits:
            events += [("i", h, k) for h in range(halves)]
        if k == 2 * hbits:
            events += [("i", h, j) for j in range(k + 1, bits + 1) for h in range(halves)]
            events += [("m",), ("j",)]
        events += [("s", p, k) for p in range(parts)]
        if k == bits + 1 and k < 2 * hbits:
            events.append(("m",))
    seen = False
    out = []
    for event in events:
        if event[0] == "m":
            if seen:
                continue
            seen = True
        out.append(event)
    return out


def put_out(*refs):
    sems = refs[6]
    copies = [pltpu.make_async_copy(refs[i], refs[3 + i], sems.at[i]) for i in range(3)]
    for copy in copies:
        copy.start()
    for copy in copies:
        copy.wait()


def body(sizes, matrix, pivot_rows, panel_perm, block_inverse):
    R, C = sizes
    rows_here, cols_here = matrix.shape
    pw = block_inverse.shape[1]
    irows = block_inverse.shape[0]
    bits = R.bit_length() - 1
    hbits = min(bits, (pw // BLOCK).bit_length() - 1)
    named = bit_orders(bits)
    names = ["xyz", "yxz", "zxy", "xyz", "yxz", "zxy", "xyz", "yxz"]
    orders = [named[n] for n in names]
    iorders = [named["xyz"], named["yxz"]]
    parts = len(orders)
    width = cols_here // parts
    NB = 1 << hbits
    share = pw // C
    left = max(1, bits - hbits)
    cap = min(rows_here, 4 * pw // R)
    firsts = len({order[0] for order in orders})
    cfg = dict(R=R, C=C, bits=bits, hbits=hbits, orders=orders, iorders=iorders, width=width,
               cap=cap, events=schedule(parts, len(iorders), bits, hbits))
    dma = pltpu.SemaphoreType.DMA
    vmem = pl.BlockSpec(memory_space=pltpu.VMEM)
    hbm = pl.BlockSpec(memory_space=pltpu.HBM)
    bf = jnp.bfloat16
    reduced, multipliers, normalized = pl.pallas_call(
        functools.partial(kernel, cfg),
        out_shape=(
            pltpu.VMEM((rows_here, cols_here), jnp.float32),
            pltpu.VMEM((rows_here, share), jnp.float32),
            pltpu.VMEM((irows, cols_here), jnp.float32),
        ),
        in_specs=[hbm, hbm, hbm, hbm],
        out_specs=(vmem, vmem, vmem),
        scratch_shapes=[
            pltpu.VMEM((1, pw), jnp.int32),
            pltpu.VMEM((1, pw), jnp.int32),
            pltpu.VMEM((irows, pw), jnp.float32),
            pltpu.VMEM((rows_here, cols_here), jnp.float32),
            pltpu.VMEM((rows_here, pw), bf),
            pltpu.VMEM((firsts, pw, cap), bf),
            pltpu.VMEM((parts, cap, width), bf),
            pltpu.VMEM((parts, cap, width), bf),
            pltpu.VMEM((parts, NB, BLOCK, width), bf),
            pltpu.VMEM((parts, NB, BLOCK, width), bf),
            pltpu.VMEM((parts, NB, BLOCK, width), bf),
            pltpu.VMEM((left, parts, BLOCK, width), bf),
            pltpu.VMEM((len(iorders), R, irows, share // len(iorders)), bf),
            pltpu.VMEM((pw, share), bf),
            pltpu.VMEM((C, rows_here, share), bf),
            pltpu.VMEM((rows_here, pw), bf),
            dma((3 + parts,)),
            dma((parts, hbits)), dma((parts, hbits)),
            dma((parts, hbits)), dma((parts, hbits)),
            dma((parts, left)), dma((parts, left)),
            dma((len(iorders), bits)), dma((len(iorders), bits)),
            dma((C,)), dma, dma((C,)), dma((C,)),
        ],
        compiler_params=pltpu.CompilerParams(
            collective_id=0, has_side_effects=True, vmem_limit_bytes=48 * 1024 * 1024
        ),
    )(*[
        pltpu.with_memory_space_constraint(x, pltpu.HBM)
        for x in (pivot_rows[None, :], panel_perm[None, :], matrix, block_inverse)
    ])
    results = (reduced, multipliers, normalized)
    return pl.pallas_call(
        put_out,
        out_shape=tuple(pltpu.HBM(x.shape, x.dtype) for x in results),
        in_specs=[vmem] * 3,
        out_specs=(hbm,) * 3,
        scratch_shapes=[dma((3,))],
    )(*[pltpu.with_memory_space_constraint(x, pltpu.VMEM) for x in results])


def solution(mesh):
    in_specs = (P("rows", "cols"), P(), P(), P("rows", None))
    out_specs = (P("rows", "cols"), P("rows", "cols"), P("rows", "cols"))
    sizes = (mesh.shape["rows"], mesh.shape["cols"])
    return jax.shard_map(
        functools.partial(body, sizes), mesh=mesh, in_specs=in_specs, out_specs=out_specs,
        check_vma=False,
    )
```

```python
import functools

import jax
import jax.numpy as jnp
from jax import lax
from jax.experimental import pallas as pl
from jax.experimental.pallas import tpu as pltpu
from jax.sharding import PartitionSpec as P

MESH = pl.DeviceIdType.MESH
MOD = 251.0
INV = 1.0 / 251.0
BLOCK = 32


def near_mod(x):
    return x - MOD * jnp.floor(x * INV)


def small_mod(x):
    return x - MOD * jnp.floor((x + 0.5) * INV)


def mod_parts(a, b):
    depth = a.shape[1]
    step = min(256, depth)
    total = None
    for k in range(0, depth, step):
        piece = near_mod(
            jnp.dot(a[:, k : k + step], b[k : k + step], preferred_element_type=jnp.float32)
        )
        total = piece if total is None else total + piece
    return total


def bit_orders(bits):
    rest = list(range(2, bits))
    return {
        "xyz": [0, 1] + rest,
        "yxz": [1, 0] + rest,
        "zxy": rest + [0, 1],
    }


def place_of(block, order):
    index = 0
    for b in order:
        index = index * 2 + ((block >> b) & 1)
    return index


def kernel(cfg, piv_hbm, perm_hbm, mat_hbm, inv_hbm, red_ref, mult_ref, norm_ref,
           piv_ref, perm_ref, inv_ref, mat, abuf, pack, packed, landed, buf, rbuf, gbuf, lbuf,
           ibuf, full_inv, mult_all, mult_half, in_sem, s_send, s_recv, g_send, g_recv, l_send, l_recv,
           i_send, i_recv, a_send, a_recv, m_send, m_recv):
    R, C, bits, hbits, orders, iorders, width, cap = (
        cfg["R"], cfg["C"], cfg["bits"], cfg["hbits"], cfg["orders"], cfg["iorders"],
        cfg["width"], cfg["cap"],
    )
    NB = 1 << hbits
    parts = len(orders)
    rows_here = mat.shape[0]
    pw = piv_ref.shape[1]
    r = lax.axis_index("rows")
    c = lax.axis_index("cols")
    fetch = [
        pltpu.make_async_copy(src, dst, in_sem.at[i])
        for i, (src, dst) in enumerate(
            [(piv_hbm, piv_ref), (inv_hbm, inv_ref), (perm_hbm, perm_ref)]
            + [
                (mat_hbm.at[:, pl.ds(p * width, width)], mat.at[:, pl.ds(p * width, width)])
                for p in range(parts)
            ]
        )
    ]
    for copy in fetch:
        copy.start()

    bit = [(r >> b) & 1 for b in range(bits)]
    partner = [r + (1 << b) * (1 - 2 * bit[b]) for b in range(bits)]

    barrier = pltpu.get_barrier_semaphore()
    for b in range(bits):
        pl.semaphore_signal(barrier, inc=1, device_id=(partner[b], c), device_id_type=MESH)
    for k in range(1, C):
        pl.semaphore_signal(barrier, inc=1, device_id=(r, lax.rem(c + k, C)), device_id_type=MESH)

    fetch[0].wait()
    piv = piv_ref[...]
    firsts = sorted({order[0] for order in orders})
    owners = [r] + [partner[b] for b in firsts]
    held = [(piv >= d * rows_here) & (piv < (d + 1) * rows_here) for d in owners]
    earlier = (
        lax.broadcasted_iota(jnp.int32, (pw, pw), 0) < lax.broadcasted_iota(jnp.int32, (pw, pw), 1)
    ).astype(jnp.bfloat16)
    flags = jnp.concatenate([h.astype(jnp.float32) for h in held], axis=0).astype(jnp.bfloat16)
    rank = jnp.dot(flags, earlier, preferred_element_type=jnp.float32).astype(jnp.int32)
    slot = lax.broadcasted_iota(jnp.int32, (cap, pw), 0)
    spots = [
        jnp.where((slot == rank[i : i + 1]) & held[i], 1.0, 0.0).astype(jnp.bfloat16)
        for i in range(len(owners))
    ]
    pick = jnp.where(
        lax.broadcasted_iota(jnp.int32, (rows_here, pw), 0) == piv - r * rows_here, 1.0, 0.0
    ).astype(jnp.bfloat16)
    pick_t = pick.T
    gather = jnp.dot(spots[0], pick_t, preferred_element_type=jnp.float32).astype(jnp.bfloat16)

    fetch[1].wait()
    inv_mine = inv_ref[...].astype(jnp.bfloat16)
    share = pw // C
    own = inv_mine[:, :share]
    for k in range(1, C):
        own = jnp.where(c == k, inv_mine[:, k * share : (k + 1) * share], own)
    iw = share // len(iorders)
    for h, order in enumerate(iorders):
        ibuf[h, place_of(r, order)] = own[:, h * iw : (h + 1) * iw]
    pl.semaphore_wait(barrier, bits + C - 1)

    def send(src, dst, ss, rs, b):
        return pltpu.make_async_remote_copy(
            src_ref=src, dst_ref=dst, send_sem=ss, recv_sem=rs,
            device_id=(partner[b], c), device_id_type=MESH,
        )

    sent = []
    flight = {}

    def go(key, copy):
        copy.start()
        sent.append(copy)
        flight[key] = copy

    def panel_copy(k):
        return pltpu.make_async_remote_copy(
            src_ref=abuf, dst_ref=abuf, send_sem=a_send.at[k], recv_sem=a_recv,
            device_id=(r, k), device_id_type=MESH,
        )

    def inv_step(h, j):
        order = iorders[h]
        if j > 0:
            flight["i", h].wait_recv()
        if j < bits:
            size = 1 << j
            base = (place_of(r, order) // size) * size
            region = ibuf.at[h, pl.ds(base, size)]
            go(("i", h), send(region, region, i_send.at[h, j], i_recv.at[h, j],
                              order[bits - 1 - j]))

    def lo_after(order, t):
        lo = 0
        for j in range(t):
            lo = lo + bit[order[j]] * (NB >> (j + 1))
        return lo

    roff = [0]
    for t in range(hbits):
        roff.append(roff[-1] + (NB >> (t + 1)))

    def slot_block(s, order):
        block = 0
        for j in range(hbits):
            block |= ((s >> (hbits - 1 - j)) & 1) << order[j]
        return block

    ranks = [sorted(range(NB), key=lambda s: slot_block(s, order)) for order in orders]

    def step(p, k):
        order = orders[p]
        cols = slice(p * width, (p + 1) * width)
        if k == 1:
            chosen = jnp.dot(
                pick_t, mat[:, cols].astype(jnp.bfloat16), preferred_element_type=jnp.float32
            )
            flight[p].wait_recv()
            chosen = chosen + jnp.dot(
                pack[firsts.index(order[0])], landed[p], preferred_element_type=jnp.float32
            )
            chosen = chosen.astype(jnp.bfloat16)
            for i in range(NB):
                buf[p, ranks[p][i]] = chosen[i * BLOCK : (i + 1) * BLOCK]
        elif 1 < k <= hbits:
            flight[p].wait_recv()
            t = k - 1
            half = NB >> k
            keep = lo_after(order, k)
            value = buf[p, pl.ds(keep, half)] + rbuf[p, pl.ds(roff[t], half)]
            if k == hbits:
                gbuf[p, pl.ds(keep, half)] = value
            else:
                buf[p, pl.ds(keep, half)] = value
        elif k > hbits:
            flight[p].wait_recv()
        if k == 0:
            fetch[3 + p].wait()
            packed[p] = jnp.dot(
                gather, mat[:, cols].astype(jnp.bfloat16), preferred_element_type=jnp.float32
            ).astype(jnp.bfloat16)
            go(p, send(packed.at[p], landed.at[p], s_send.at[p, 0], s_recv.at[p, 0], order[0]))
        elif k < hbits:
            half = NB >> (k + 1)
            away = lo_after(order, k) + (1 - bit[order[k]]) * half
            go(p, send(buf.at[p, pl.ds(away, half)], rbuf.at[p, pl.ds(roff[k], half)],
                       s_send.at[p, k], s_recv.at[p, k], order[k]))
        elif k < 2 * hbits:
            if k == hbits:
                keep = lo_after(order, hbits)
                for j, b in enumerate(order[hbits:]):
                    copy = send(gbuf.at[p, keep], lbuf.at[j, p], l_send.at[p, j],
                                l_recv.at[p, j], b)
                    copy.start()
                    copy.wait()
                    gbuf[p, keep] = gbuf[p, keep] + lbuf[j, p]
            t = 2 * hbits - 1 - k
            region = gbuf.at[p, pl.ds(lo_after(order, t + 1), NB >> (t + 1))]
            go(p, send(region, region, g_send.at[p, t], g_recv.at[p, t], order[t]))
        else:
            slab = jnp.concatenate([gbuf[p, ranks[p][i]] for i in range(NB)], axis=0)
            red_ref[:, cols] = small_mod(mat[:, cols] - mod_parts(mult_half[...], slab))
            norm_ref[:, cols] = small_mod(mod_parts(inv_mine, slab))

    def multipliers():
        irows = pw // R
        for h, order in enumerate(iorders):
            for i in range(R):
                full_inv[i * irows : (i + 1) * irows, h * iw : (h + 1) * iw] = ibuf[
                    h, place_of(i, order)
                ]

        @pl.when(c != 0)
        def _():
            panel_copy(0).wait_recv()

        fetch[2].wait()
        turn = jnp.where(
            lax.broadcasted_iota(jnp.int32, (pw, pw), 0) == perm_ref[...], 1.0, 0.0
        ).astype(jnp.bfloat16)
        turned = jnp.dot(turn, full_inv[...], preferred_element_type=jnp.float32)
        mult = small_mod(mod_parts(abuf[...], turned.astype(jnp.bfloat16)))
        mult_ref[...] = mult
        mult_all[c] = mult.astype(jnp.bfloat16)
        for k in range(1, C):
            swap(k).start()

    def swap(k):
        return pltpu.make_async_remote_copy(
            src_ref=mult_all.at[c], dst_ref=mult_all.at[c], send_sem=m_send.at[k],
            recv_sem=m_recv.at[k], device_id=(r, lax.rem(c + k, C)), device_id_type=MESH,
        )

    def join():
        for k in range(1, C):
            swap(k).wait()
        for k in range(C):
            mult_half[:, k * share : (k + 1) * share] = mult_all[k]

    for event in cfg["events"]:
        if event[0] == "i":
            inv_step(event[1], event[2])
        elif event[0] == "a":
            @pl.when(c == 0)
            def _():
                abuf[...] = mat[:, :pw].astype(jnp.bfloat16)

            for k in range(1, C):
                @pl.when(c == 0)
                def _():
                    panel_copy(k).start()
        elif event[0] == "u":
            for i in range(len(firsts)):
                pack[i] = spots[i + 1].T
        elif event[0] == "m":
            multipliers()
        elif event[0] == "j":
            join()
        else:
            step(event[1], event[2])

    for copy in sent:
        copy.wait_send()
    for k in range(1, C):
        @pl.when(c == 0)
        def _():
            panel_copy(k).wait_send()


def schedule(parts, halves, bits, hbits):
    events = [("i", h, 0) for h in range(halves)]
    events += [("s", p, 0) for p in range(parts)] + [("a",), ("u",)]
    for k in range(1, 2 * hbits + 1):
        if k <= bits:
            events += [("i", h, k) for h in range(halves)]
        if k == 2 * hbits:
            events += [("i", h, j) for j in range(k + 1, bits + 1) for h in range(halves)]
            events += [("m",), ("j",)]
        events += [("s", p, k) for p in range(parts)]
        if k == bits + 1 and k < 2 * hbits:
            events.append(("m",))
    seen = False
    out = []
    for event in events:
        if event[0] == "m":
            if seen:
                continue
            seen = True
        out.append(event)
    return out


def put_out(*refs):
    sems = refs[6]
    copies = [pltpu.make_async_copy(refs[i], refs[3 + i], sems.at[i]) for i in range(3)]
    for copy in copies:
        copy.start()
    for copy in copies:
        copy.wait()


def body(sizes, matrix, pivot_rows, panel_perm, block_inverse):
    R, C = sizes
    rows_here, cols_here = matrix.shape
    pw = block_inverse.shape[1]
    irows = block_inverse.shape[0]
    bits = R.bit_length() - 1
    hbits = min(bits, (pw // BLOCK).bit_length() - 1)
    named = bit_orders(bits)
    names = ["xyz", "yxz", "zxy", "xyz", "yxz", "zxy", "xyz", "yxz"]
    orders = [named[n] for n in names]
    iorders = [named["xyz"], named["yxz"]]
    parts = len(orders)
    width = cols_here // parts
    NB = 1 << hbits
    share = pw // C
    left = max(1, bits - hbits)
    cap = min(rows_here, 4 * pw // R)
    firsts = len({order[0] for order in orders})
    cfg = dict(R=R, C=C, bits=bits, hbits=hbits, orders=orders, iorders=iorders, width=width,
               cap=cap, events=schedule(parts, len(iorders), bits, hbits))
    dma = pltpu.SemaphoreType.DMA
    vmem = pl.BlockSpec(memory_space=pltpu.VMEM)
    hbm = pl.BlockSpec(memory_space=pltpu.HBM)
    bf = jnp.bfloat16
    reduced, multipliers, normalized = pl.pallas_call(
        functools.partial(kernel, cfg),
        out_shape=(
            pltpu.VMEM((rows_here, cols_here), jnp.float32),
            pltpu.VMEM((rows_here, share), jnp.float32),
            pltpu.VMEM((irows, cols_here), jnp.float32),
        ),
        in_specs=[hbm, hbm, hbm, hbm],
        out_specs=(vmem, vmem, vmem),
        scratch_shapes=[
            pltpu.VMEM((1, pw), jnp.int32),
            pltpu.VMEM((1, pw), jnp.int32),
            pltpu.VMEM((irows, pw), jnp.float32),
            pltpu.VMEM((rows_here, cols_here), jnp.float32),
            pltpu.VMEM((rows_here, pw), bf),
            pltpu.VMEM((firsts, pw, cap), bf),
            pltpu.VMEM((parts, cap, width), bf),
            pltpu.VMEM((parts, cap, width), bf),
            pltpu.VMEM((parts, NB, BLOCK, width), bf),
            pltpu.VMEM((parts, NB, BLOCK, width), bf),
            pltpu.VMEM((parts, NB, BLOCK, width), bf),
            pltpu.VMEM((left, parts, BLOCK, width), bf),
            pltpu.VMEM((len(iorders), R, irows, share // len(iorders)), bf),
            pltpu.VMEM((pw, share), bf),
            pltpu.VMEM((C, rows_here, share), bf),
            pltpu.VMEM((rows_here, pw), bf),
            dma((3 + parts,)),
            dma((parts, hbits)), dma((parts, hbits)),
            dma((parts, hbits)), dma((parts, hbits)),
            dma((parts, left)), dma((parts, left)),
            dma((len(iorders), bits)), dma((len(iorders), bits)),
            dma((C,)), dma, dma((C,)), dma((C,)),
        ],
        compiler_params=pltpu.CompilerParams(
            collective_id=0, has_side_effects=True, vmem_limit_bytes=48 * 1024 * 1024
        ),
    )(*[
        pltpu.with_memory_space_constraint(x, pltpu.HBM)
        for x in (pivot_rows[None, :], panel_perm[None, :], matrix, block_inverse)
    ])
    results = (reduced, multipliers, normalized)
    return pl.pallas_call(
        put_out,
        out_shape=tuple(pltpu.HBM(x.shape, x.dtype) for x in results),
        in_specs=[vmem] * 3,
        out_specs=(hbm,) * 3,
        scratch_shapes=[dma((3,))],
    )(*[pltpu.with_memory_space_constraint(x, pltpu.VMEM) for x in results])


def solution(mesh):
    in_specs = (P("rows", "cols"), P(), P(), P("rows", None))
    out_specs = (P("rows", "cols"), P("rows", "cols"), P("rows", "cols"))
    sizes = (mesh.shape["rows"], mesh.shape["cols"])
    return jax.shard_map(
        functools.partial(body, sizes), mesh=mesh, in_specs=in_specs, out_specs=out_specs,
        check_vma=False,
    )
```
